32 devices in a mesh: orb: 4 (over z), box: 8 (over y, x, core).
Axes of the slice: x: 2, y: 2, z: 4, core: 2. Of those that a mesh axis runs over, the one named last changes fastest.
Arguments:
- coarse: bfloat16 [4, 8, 729, 1024], P('orb', None, None, 'box'), may hold values from -1.5 to 1.5
- wavelets: bfloat16 [4, 7, 729, 1024], P('orb', None, None, 'box'), may hold values from -1.5 to 1.5
- leaf_flags: int32 [4, 1024], P('orb', 'box'), may hold values 0 or 1
- child_key1: int32 [1024], P('box'), may hold values from 0 to 8191, as said below
- child_key2: int32 [2048], P('box'), may hold values from 0 to 8191, as said below
- counts: int32 [8], P('box'), may hold values from 128 to 256, as said below
Outputs:
- density: float32 [729, 2048], P(None, 'box')
The draws below stay inside these ranges and needn't reach their ends.
Inputs may be any that keep to these rules, and one draw needn't show every extreme that they name: `child_key1`: within each curve range of 128 entries the keys rise and name distinct children; each parent lies in the same range or among the last 32 boxes of the range before; every range but the first has an entry naming a child of the first of those 32 boxes. `child_key2`: within each curve range of 256 entries the keys rise and name distinct children; each parent lies in the same range or among the last 32 boxes of the range before; every range but the first has an entry naming a child of the first of those 32 boxes. `counts`: some range is full in every draw and some range holds the fewest.
All inputs are finite; a program needn't handle non-finite values. No bound on the sum of `leaf_flags` on one device may be relied on, other than what follows from the above.
Results may differ from the reference program's by a relative error of at most 0.0003.
Values may be sent and summed in bfloat16 or wider, within the bound.
A program may use at most 64 MiB of HBM per device.

```python
import math
import jax
import jax.numpy as jnp
import numpy as np
from jax import lax

BOX_DEV = 128
ORBITALS = 4
BOXES = 1024
LEAVES = 2048
SPILL = 32


def range_keys(key, slots):
    ranges = BOXES // BOX_DEV
    margin = 8 * SPILL
    choices_all = 8 * (BOX_DEV + SPILL)
    choices_first = 8 * BOX_DEV

    def one_range(position):
        folded = jax.random.fold_in(key, position)
        key_rest, key_first = jax.random.split(folded)
        middle = 1 + jax.random.permutation(key_rest, choices_all - 2)[:slots - 2]
        picked = jnp.concatenate([jnp.zeros((1,), jnp.int32), middle.astype(jnp.int32), jnp.full((1,), choices_all - 1, jnp.int32)])
        earlier = picked < margin
        shifted = picked - margin
        parent = jnp.where(earlier, (position - 1) * BOX_DEV + BOX_DEV - SPILL + picked // 8, position * BOX_DEV + shifted // 8)
        octant = jnp.where(earlier, picked % 8, shifted % 8)
        general = 8 * parent + octant
        middle_first = 1 + jax.random.permutation(key_first, choices_first - 2)[:slots - 2]
        first_codes = jnp.concatenate([jnp.zeros((1,), jnp.int32), middle_first.astype(jnp.int32), jnp.full((1,), choices_first - 1, jnp.int32)])
        codes = jnp.where(position == 0, first_codes, general)
        return jnp.sort(codes)
    return jax.vmap(one_range)(jnp.arange(ranges, dtype=jnp.int32)).reshape(-1).astype(jnp.int32)


def draw_child_key1(key, part):
    return range_keys(jax.random.fold_in(key, 11), BOX_DEV)


def draw_child_key2(key, part):
    return range_keys(jax.random.fold_in(key, 23), 2 * BOX_DEV)


def draw_counts(key, part):
    ranges = BOXES // BOX_DEV
    key_all, key_full, key_low = jax.random.split(jax.random.fold_in(key, 37), 3)
    values = jax.random.randint(key_all, (ranges,), BOX_DEV, 2 * BOX_DEV + 1, dtype=jnp.int32)
    fullest = jax.random.randint(key_full, (), 0, ranges, dtype=jnp.int32)
    lowest = (fullest + 1 + jax.random.randint(key_low, (), 0, ranges - 1, dtype=jnp.int32)) % ranges
    positions = jnp.arange(ranges, dtype=jnp.int32)
    values = jnp.where(positions == fullest, 2 * BOX_DEV, values)
    values = jnp.where(positions == lowest, BOX_DEV, values)
    return values.astype(jnp.int32)


def place_ends(values, stream_key, least, top_value):
    index_at = [jax.random.randint(jax.random.fold_in(stream_key, axis), (), 0, length) for axis, length in enumerate(values.shape)]
    widest = values.shape.index(max(values.shape))
    next_to = index_at[:widest] + [(index_at[widest] + 1) % values.shape[widest]] + index_at[widest + 1:]
    return values.at[tuple(index_at)].set(least).at[tuple(next_to)].set(top_value)


def levels(rng, shape, pieces, low, largest):
    loudness, own = 1.0, jax.random.fold_in(rng, 6)
    for dim, parts in pieces:
        draws = jnp.exp(jax.random.uniform(jax.random.fold_in(own, dim), (parts,), jnp.float32, low / len(pieces), largest / len(pieces)))
        loudness = loudness * jnp.repeat(draws, shape[dim] // parts).reshape([-1 if axis == dim else 1 for axis in range(len(shape))])
    return loudness


def normal_values(key, dims, scale, reach, pieces=(), kind=jnp.bfloat16):
    values = jax.random.normal(key, dims, jnp.float32) * scale
    if len(pieces) > 0:
        values = levels(key, dims, pieces, -0.22, 0.18) * values
    return jnp.clip(values, min=-reach, max=reach).astype(kind)


def setup_inputs(seed: int = 0) -> dict:
    splits = jax.random.split(jax.random.key(seed), 7)
    return {
        "coarse": normal_values(splits[0], (ORBITALS, 8, 729, BOXES), 0.25, 1.5, ((0, 4), (3, 8))),
        "wavelets": normal_values(splits[1], (ORBITALS, 7, 729, BOXES), 0.25, 1.5, ((0, 4), (3, 8))),
        "leaf_flags": place_ends((jax.random.randint(splits[2], (ORBITALS, BOXES), 0, 2) < 1).astype(jnp.int32), jax.random.fold_in(splits[2], 1), 0, 1),
        "child_key1": draw_child_key1(jax.random.fold_in(splits[6], 71), 0),
        "child_key2": draw_child_key2(jax.random.fold_in(splits[6], 71), 0),
        "counts": draw_counts(jax.random.fold_in(splits[6], 71), 0),
    }


def legendre_pair(order, where):
    before = where * 0.0 + 1.0
    value = where
    for degree in range(1, order):
        before, value = (value, ((2 * degree + 1) * where * value - degree * before) / (degree + 1))
    return (value, before)

def gauss_rule(order):
    nodes = np.cos(np.pi * (np.arange(order) + 0.75) / (order + 0.5))
    for repeat in range(40):
        value, before = legendre_pair(order, nodes)
        slope = order * (nodes * value - before) / (nodes * nodes - 1.0)
        nodes = nodes - value / slope
    value, before = legendre_pair(order, nodes)
    slope = order * (nodes * value - before) / (nodes * nodes - 1.0)
    weights = 2.0 / ((1.0 - nodes * nodes) * slope * slope)
    return (nodes[::-1], weights[::-1])

def legendre_basis(where):
    shifted = 2.0 * where - 1.0
    rows = [shifted * 0.0 + 1.0, shifted]
    for degree in range(1, 8):
        rows.append(((2 * degree + 1) * shifted * rows[degree] - degree * rows[degree - 1]) / (degree + 1))
    scale = np.sqrt(2.0 * np.arange(9) + 1.0)[:, None]
    return np.stack(rows, 0) * scale

def complement_rows(scaling_rows):
    members = [scaling_rows[index] for index in range(9)]
    kept = []
    identity = np.eye(18)
    for column in range(18):
        vector = identity[column]
        for passes in range(2):
            for member in members + kept:
                vector = vector - np.dot(member, vector) * member
        length = np.sqrt(np.dot(vector, vector))
        if length > 0.1 and len(kept) < 9:
            kept.append(vector / length)
    return np.stack(kept, 0)

def wavelet_tables():
    nodes, weights = gauss_rule(24)
    points = 0.5 * (nodes + 1.0)
    halves = 0.5 * weights
    lower = legendre_basis(0.5 * points) * halves @ legendre_basis(points).T / math.sqrt(2.0)
    upper = legendre_basis(0.5 * points + 0.5) * halves @ legendre_basis(points).T / math.sqrt(2.0)
    scaling_rows = np.concatenate([lower, upper], 1)
    wavelet_rows = complement_rows(scaling_rows)
    matrix = np.concatenate([scaling_rows, wavelet_rows], 0).reshape(2, 9, 2, 9)
    gauss, gauss_weights = gauss_rule(9)
    quad = legendre_basis(0.5 * (gauss + 1.0)).T * np.sqrt(0.5 * gauss_weights)[:, None]
    return (jnp.asarray(matrix, dtype=jnp.float32), jnp.asarray(quad, dtype=jnp.float32))

def expand(blocks, filters):
    highest = lax.Precision.HIGHEST
    cube = blocks.reshape(2, 2, 2, 9, 9, 9, -1)
    cube = jnp.einsum('abcijlz,aiod->bcjlodz', cube, filters, precision=highest)
    cube = jnp.einsum('bcjlodz,bjqe->clodqez', cube, filters, precision=highest)
    cube = jnp.einsum('clodqez,clrf->defoqrz', cube, filters, precision=highest)
    return cube.reshape(729, 8, -1)

def select(children, codes):
    width = children.shape[2]
    flat = children.reshape(729, 8 * width)
    index = (codes % 8 * width + codes // 8).astype(jnp.int32)
    return jnp.take(flat, index, axis=1)

def quadrature(scaling, quad):
    highest = lax.Precision.HIGHEST
    cube = scaling.reshape(9, 9, 9, -1)
    cube = jnp.einsum('ijlz,gi->gjlz', cube, quad, precision=highest)
    cube = jnp.einsum('gjlz,hj->ghlz', cube, quad, precision=highest)
    cube = jnp.einsum('ghlz,kl->ghkz', cube, quad, precision=highest)
    return cube.reshape(729, -1)

def reference(coarse, wavelets, leaf_flags, child_key1, child_key2, counts):
    filters, quad = wavelet_tables()

    def orbital_step(total, items):
        coarse_one, wave_one, leaf_one = items
        children = expand(coarse_one.astype(jnp.float32), filters)
        first = select(children, child_key1)
        keep = (1 - leaf_one).astype(jnp.float32)
        blocks = jnp.concatenate([first[None], wave_one.astype(jnp.float32) * keep], 0)
        children = expand(blocks, filters)
        second = select(children, child_key2)
        values = quadrature(second, quad)
        return (total + values * values, None)
    start = jnp.zeros((729, LEAVES), jnp.float32)
    total, unused = lax.scan(orbital_step, start, (coarse, wavelets, leaf_flags))
    slots = jnp.arange(LEAVES, dtype=jnp.int32)
    live = slots % (2 * BOX_DEV) < counts[slots // (2 * BOX_DEV)]
    return 2.0 * total * live.astype(jnp.float32)
```

```python
import math

import jax
import jax.numpy as jnp
import numpy as np
from jax import lax
from jax.experimental import pallas as pl
from jax.experimental.pallas import tpu as pltpu
from jax.sharding import PartitionSpec as P

SPILL = 32


def shifted_2(value, axis, steps):
    count = lax.axis_size(axis)
    first, last = (max(0, -steps), min(count, count - steps))
    return lax.ppermute(value, axis, [(source, source + steps) for source in range(first, last)])


def legendre_pair(order, where):
    before = where * 0.0 + 1.0
    value = where
    for degree in range(1, order):
        before, value = (value, ((2 * degree + 1) * where * value - degree * before) / (degree + 1))
    return (value, before)


def gauss_rule(order):
    nodes = np.cos(np.pi * (np.arange(order) + 0.75) / (order + 0.5))
    for repeat in range(40):
        value, before = legendre_pair(order, nodes)
        slope = order * (nodes * value - before) / (nodes * nodes - 1.0)
        nodes = nodes - value / slope
    value, before = legendre_pair(order, nodes)
    slope = order * (nodes * value - before) / (nodes * nodes - 1.0)
    weights = 2.0 / ((1.0 - nodes * nodes) * slope * slope)
    return (nodes[::-1], weights[::-1])


def legendre_basis(where):
    shifted = 2.0 * where - 1.0
    rows = [shifted * 0.0 + 1.0, shifted]
    for degree in range(1, 8):
        rows.append(
            ((2 * degree + 1) * shifted * rows[degree] - degree * rows[degree - 1]) / (degree + 1)
        )
    scale = np.sqrt(2.0 * np.arange(9) + 1.0)[:, None]
    return np.stack(rows, 0) * scale


def complement_rows(scaling_rows):
    members = [scaling_rows[index] for index in range(9)]
    kept = []
    identity = np.eye(18)
    for column in range(18):
        vector = identity[column]
        for passes in range(2):
            for member in members + kept:
                vector = vector - np.dot(member, vector) * member
        length = np.sqrt(np.dot(vector, vector))
        if length > 0.1 and len(kept) < 9:
            kept.append(vector / length)
    return np.stack(kept, 0)


def wavelet_tables():
    nodes, weights = gauss_rule(24)
    points = 0.5 * (nodes + 1.0)
    halves = 0.5 * weights
    lower = legendre_basis(0.5 * points) * halves @ legendre_basis(points).T / math.sqrt(2.0)
    upper = legendre_basis(0.5 * points + 0.5) * halves @ legendre_basis(points).T / math.sqrt(2.0)
    scaling_rows = np.concatenate([lower, upper], 1)
    wavelet_rows = complement_rows(scaling_rows)
    matrix = np.concatenate([scaling_rows, wavelet_rows], 0).reshape(2, 9, 2, 9)
    gauss, gauss_weights = gauss_rule(9)
    quad = legendre_basis(0.5 * (gauss + 1.0)).T * np.sqrt(0.5 * gauss_weights)[:, None]
    return (matrix.reshape(18, 2, 9), quad)


ROWS = 729
PADDED = 800
GROUPS = ((0, 1), (2, 3), (4, 5), (6, 7), (8, 9, 10))
QUARTER = 192


def local_keys(key_ref, boxes):
    key = key_ref[...] - lax.axis_index("box") * (8 * boxes)
    return (lax.shift_right_arithmetic(key, 3), key & 7)


def spread_matrix(boxes, group):
    source = lax.broadcasted_iota(jnp.int32, (boxes, 128), 0)
    target = lax.broadcasted_iota(jnp.int32, (boxes, 128), 1)
    hit = (source - (boxes - SPILL) == target - SPILL * group) & (source >= boxes - SPILL)
    return hit.astype(jnp.float32).astype(jnp.bfloat16)


def pick_own(column, boxes):
    row = lax.broadcasted_iota(jnp.int32, (boxes, column.shape[1]), 0)
    return (row == column).astype(jnp.float32)


def pick_spilled(column, group):
    row = lax.broadcasted_iota(jnp.int32, (128, column.shape[1]), 0)
    hit = (row == column + SPILL * (group + 1)) & (column < 0)
    return hit.astype(jnp.float32)


def fill_coefficients(coef_ref, octant, table):
    for axis in range(3):
        bit = jnp.broadcast_to((octant >> axis) & 1, (8, 128)) == 1
        for k in range(18):
            for f in range(9):
                coef_ref[axis * 162 + k * 9 + f] = jnp.where(
                    bit, np.float32(table[k, 1, f]), np.float32(table[k, 0, f])
                )


def contract(source_ref, low, high, coef_ref, axis, store):
    for group in GROUPS:
        inputs = [
            [
                source_ref[block, pl.ds(l + 72 * t, 8, stride=9), :]
                for block in (low, high)
                for l in range(9)
            ]
            for t in group
        ]
        for f in range(9):
            sums = [None] * len(group)
            for k in range(18):
                weight = coef_ref[axis * 162 + k * 9 + f]
                for n in range(len(group)):
                    term = weight * inputs[n][k]
                    sums[n] = term if sums[n] is None else sums[n] + term
            for n, t in enumerate(group):
                store(81 * f + 8 * t, min(8, 81 - 8 * t), sums[n])


def transform(x_ref, a_ref, b_ref, coef_ref, finish):
    def first(index, carry):
        def store(row, count, value):
            a_ref[index, row : row + count, :] = value[:count]

        contract(x_ref, 2 * index, 2 * index + 1, coef_ref, 0, store)
        return carry

    lax.fori_loop(0, 4, first, 0)

    def second(index, carry):
        def store(row, count, value):
            b_ref[index, row : row + count, :] = value[:count]

        contract(a_ref, 2 * index, 2 * index + 1, coef_ref, 1, store)
        return carry

    lax.fori_loop(0, 2, second, 0)
    contract(b_ref, 0, 1, coef_ref, 2, finish)


def dot(left, right):
    return jnp.dot(left, right, preferred_element_type=jnp.float32)


def pack_coarse_kernel(coarse_ref, out_ref):
    boxes = coarse_ref.shape[-1]
    spread = [spread_matrix(boxes, g) for g in range(4)]
    for h in range(2):
        total = dot(coarse_ref[h], spread[0])
        for g in range(1, 4):
            total = total + dot(coarse_ref[2 * g + h], spread[g])
        out_ref[h] = total.astype(jnp.bfloat16)


def pack_waves_kernel(waves_ref, flags_ref, out_ref):
    boxes = waves_ref.shape[-1]
    keep = (1 - flags_ref[...]).astype(jnp.float32)
    source = lax.broadcasted_iota(jnp.int32, (128, SPILL), 0)
    spread = [spread_matrix(boxes, g) for g in range(4)]
    packed_keep = sum(dot(jnp.broadcast_to(keep, (16, boxes)).astype(jnp.bfloat16), s) for s in spread)
    packed_keep = packed_keep[:1]
    for h in range(2):
        total = jnp.zeros((ROWS, 128), jnp.float32)
        for g in range(4):
            if 2 * g + h > 0:
                total = total + dot(waves_ref[2 * g + h - 1], spread[g])
        out_ref[h] = (total * packed_keep).astype(jnp.bfloat16)


def first_kernel(coarse_ref, halo_ref, key_ref, s_ref, spill_ref, x_ref, a_ref, b_ref, coef_ref, fine_ref, *, table):
    boxes = coarse_ref.shape[-1]
    column, octant = local_keys(key_ref, boxes)
    fill_coefficients(coef_ref, octant, table)
    own = pick_own(column, boxes)
    for g in range(4):
        pick = jnp.concatenate([own, pick_spilled(column, g)], 0).astype(jnp.bfloat16)
        for h in range(2):
            both = jnp.concatenate([coarse_ref[2 * g + h], halo_ref[h]], 1)
            x_ref[2 * g + h, 0:ROWS, :] = dot(both, pick)
    fine_ref[ROWS - 1 : 4 * QUARTER, :] = jnp.zeros((4 * QUARTER - ROWS + 1, 128), jnp.float32)

    def store(row, count, value):
        fine_ref[row : row + count, :] = value[:count]

    transform(x_ref, a_ref, b_ref, coef_ref, store)
    fine = fine_ref[...]
    high = fine.astype(jnp.bfloat16)
    low = (fine - high.astype(jnp.float32)).astype(jnp.bfloat16)
    s_ref[0] = high
    s_ref[1] = low
    for part, whole in enumerate((high, low)):
        total = None
        for g in range(4):
            term = dot(whole[QUARTER * g : QUARTER * (g + 1)], spread_matrix(boxes, g))
            total = term if total is None else total + term
        spill_ref[part] = total.astype(jnp.bfloat16)


def second_kernel(
    counts_ref, waves_ref, halo_ref, flags_ref, s_ref, spill_ref, key_ref, out_ref, x_ref, a_ref, b_ref, coef_ref, *, table
):
    boxes = waves_ref.shape[-1]
    column, octant = local_keys(key_ref, boxes)
    fill_coefficients(coef_ref, octant, table)
    own = pick_own(column, boxes)
    keep = (1 - flags_ref[...]).astype(jnp.float32)
    kept = dot(jnp.broadcast_to(keep, (16, boxes)).astype(jnp.bfloat16), own.astype(jnp.bfloat16))
    own_kept = own * kept[:1]
    for g in range(4):
        spilled = pick_spilled(column, g)
        pick = jnp.concatenate([own, spilled], 0).astype(jnp.bfloat16)
        total = None
        for part in range(2):
            both = jnp.concatenate([s_ref[part, QUARTER * g : QUARTER * (g + 1), :], spill_ref[part]], 1)
            term = dot(both, pick)
            total = term if total is None else total + term
        x_ref[0, QUARTER * g : QUARTER * (g + 1), :] = total
        pick = jnp.concatenate([own_kept, spilled], 0).astype(jnp.bfloat16)
        for h in range(2):
            if 2 * g + h > 0:
                both = jnp.concatenate([waves_ref[2 * g + h - 1], halo_ref[h]], 1)
                x_ref[2 * g + h, 0:ROWS, :] = dot(both, pick)
    slot = pl.program_id(0) * 128 + lax.broadcasted_iota(jnp.int32, (8, 128), 1)
    live = jnp.where(slot < counts_ref[0], 2.0, 0.0).astype(jnp.float32)

    def store(row, count, value):
        out_ref[row : row + count, :] = (value * value * live)[:count]

    transform(x_ref, a_ref, b_ref, coef_ref, store)


def transform_scratch():
    return [
        pltpu.VMEM((8, PADDED, 128), jnp.float32),
        pltpu.VMEM((4, PADDED, 128), jnp.float32),
        pltpu.VMEM((2, PADDED, 128), jnp.float32),
        pltpu.VMEM((3 * 162, 8, 128), jnp.float32),
    ]


def shards(coarse, wavelets, leaf_flags, child_key1, child_key2, counts):
    matrix, quad = wavelet_tables()
    valued = np.einsum("kop,gp->kog", matrix, quad)
    boxes = coarse.shape[-1]
    slots = child_key2.shape[0]
    vmem = pl.BlockSpec(memory_space=pltpu.VMEM)
    packed = jax.ShapeDtypeStruct((2, ROWS, 128), jnp.bfloat16)
    coarse, wavelets = coarse[0], wavelets[0]
    params = pltpu.CompilerParams(vmem_limit_bytes=48 * 1024 * 1024)
    coarse_halo = pl.pallas_call(
        pack_coarse_kernel, out_shape=packed, in_specs=[vmem], out_specs=vmem, compiler_params=params
    )(coarse)
    coarse_halo = shifted_2(coarse_halo, "box", 1)
    waves_halo = pl.pallas_call(
        pack_waves_kernel, out_shape=packed, in_specs=[vmem] * 2, out_specs=vmem, compiler_params=params
    )(wavelets, leaf_flags)
    waves_halo = shifted_2(waves_halo, "box", 1)
    scaling, spill = pl.pallas_call(
        lambda *refs: first_kernel(*refs, table=matrix),
        out_shape=(
            jax.ShapeDtypeStruct((2, 4 * QUARTER, 128), jnp.bfloat16),
            jax.ShapeDtypeStruct((2, QUARTER, 128), jnp.bfloat16),
        ),
        in_specs=[vmem] * 3,
        out_specs=(vmem, vmem),
        scratch_shapes=transform_scratch() + [pltpu.VMEM((4 * QUARTER, 128), jnp.float32)],
        compiler_params=params,
    )(coarse, coarse_halo, child_key1.reshape(1, boxes))
    spill = shifted_2(spill, "box", 1)

    def whole(shape):
        return pl.BlockSpec(shape, lambda step: (0,) * len(shape))

    partial_density = pl.pallas_call(
        lambda *refs: second_kernel(*refs, table=valued),
        grid=(slots // 128,),
        out_shape=jax.ShapeDtypeStruct((ROWS, slots), jnp.float32),
        in_specs=[
            pl.BlockSpec(memory_space=pltpu.SMEM),
            whole(wavelets.shape),
            whole(packed.shape),
            whole(leaf_flags.shape),
            whole(scaling.shape),
            whole(spill.shape),
            pl.BlockSpec((1, 128), lambda step: (0, step)),
        ],
        out_specs=pl.BlockSpec((ROWS, 128), lambda step: (0, step)),
        scratch_shapes=transform_scratch(),
        compiler_params=params,
    )(counts, wavelets, waves_halo, leaf_flags, scaling, spill, child_key2.reshape(1, slots))
    return lax.psum(partial_density, "orb")


def solution(mesh):
    in_specs = (
        P("orb", None, None, "box"),
        P("orb", None, None, "box"),
        P("orb", "box"),
        P("box"),
        P("box"),
        P("box"),
    )
    out_specs = P(None, "box")
    return jax.shard_map(shards, mesh=mesh, in_specs=in_specs, out_specs=out_specs, check_vma=False)
```

```python
import math

import jax
import jax.numpy as jnp
import numpy as np
from jax import lax
from jax.experimental import pallas as pl
from jax.experimental.pallas import tpu as pltpu
from jax.sharding import PartitionSpec as P

SPILL = 32


def shifted_2(value, axis, steps):
    count = lax.axis_size(axis)
    first, last = (max(0, -steps), min(count, count - steps))
    return lax.ppermute(value, axis, [(source, source + steps) for source in range(first, last)])


def legendre_pair(order, where):
    before = where * 0.0 + 1.0
    value = where
    for degree in range(1, order):
        before, value = (value, ((2 * degree + 1) * where * value - degree * before) / (degree + 1))
    return (value, before)


def gauss_rule(order):
    nodes = np.cos(np.pi * (np.arange(order) + 0.75) / (order + 0.5))
    for repeat in range(40):
        value, before = legendre_pair(order, nodes)
        slope = order * (nodes * value - before) / (nodes * nodes - 1.0)
        nodes = nodes - value / slope
    value, before = legendre_pair(order, nodes)
    slope = order * (nodes * value - before) / (nodes * nodes - 1.0)
    weights = 2.0 / ((1.0 - nodes * nodes) * slope * slope)
    return (nodes[::-1], weights[::-1])


def legendre_basis(where):
    shifted = 2.0 * where - 1.0
    rows = [shifted * 0.0 + 1.0, shifted]
    for degree in range(1, 8):
        rows.append(
            ((2 * degree + 1) * shifted * rows[degree] - degree * rows[degree - 1]) / (degree + 1)
        )
    scale = np.sqrt(2.0 * np.arange(9) + 1.0)[:, None]
    return np.stack(rows, 0) * scale


def complement_rows(scaling_rows):
    members = [scaling_rows[index] for index in range(9)]
    kept = []
    identity = np.eye(18)
    for column in range(18):
        vector = identity[column]
        for passes in range(2):
            for member in members + kept:
                vector = vector - np.dot(member, vector) * member
        length = np.sqrt(np.dot(vector, vector))
        if length > 0.1 and len(kept) < 9:
            kept.append(vector / length)
    return np.stack(kept, 0)


def wavelet_tables():
    nodes, weights = gauss_rule(24)
    points = 0.5 * (nodes + 1.0)
    halves = 0.5 * weights
    lower = legendre_basis(0.5 * points) * halves @ legendre_basis(points).T / math.sqrt(2.0)
    upper = legendre_basis(0.5 * points + 0.5) * halves @ legendre_basis(points).T / math.sqrt(2.0)
    scaling_rows = np.concatenate([lower, upper], 1)
    wavelet_rows = complement_rows(scaling_rows)
    matrix = np.concatenate([scaling_rows, wavelet_rows], 0).reshape(2, 9, 2, 9)
    gauss, gauss_weights = gauss_rule(9)
    quad = legendre_basis(0.5 * (gauss + 1.0)).T * np.sqrt(0.5 * gauss_weights)[:, None]
    return (matrix.reshape(18, 2, 9), quad)


ROWS = 729
PADDED = 800
GROUPS = ((0, 1), (2, 3), (4, 5), (6, 7), (8, 9, 10))
QUARTER = 192


def local_keys(key_ref, boxes):
    key = key_ref[...] - lax.axis_index("box") * (8 * boxes)
    return (lax.shift_right_arithmetic(key, 3), key & 7)


def spread_matrix(boxes, group):
    source = lax.broadcasted_iota(jnp.int32, (boxes, 128), 0)
    target = lax.broadcasted_iota(jnp.int32, (boxes, 128), 1)
    hit = (source - (boxes - SPILL) == target - SPILL * group) & (source >= boxes - SPILL)
    return hit.astype(jnp.float32).astype(jnp.bfloat16)


def pick_own(column, boxes):
    row = lax.broadcasted_iota(jnp.int32, (boxes, column.shape[1]), 0)
    return (row == column).astype(jnp.float32)


def pick_spilled(column, group):
    row = lax.broadcasted_iota(jnp.int32, (128, column.shape[1]), 0)
    hit = (row == column + SPILL * (group + 1)) & (column < 0)
    return hit.astype(jnp.float32)


def fill_coefficients(coef_ref, octant, table):
    for axis in range(3):
        bit = jnp.broadcast_to((octant >> axis) & 1, (8, 128)) == 1
        for k in range(18):
            for f in range(9):
                coef_ref[axis * 162 + k * 9 + f] = jnp.where(
                    bit, np.float32(table[k, 1, f]), np.float32(table[k, 0, f])
                )


def contract(source_ref, low, high, coef_ref, axis, store):
    for group in GROUPS:
        inputs = [
            [
                source_ref[block, pl.ds(l + 72 * t, 8, stride=9), :]
                for block in (low, high)
                for l in range(9)
            ]
            for t in group
        ]
        for f in range(9):
            sums = [None] * len(group)
            for k in range(18):
                weight = coef_ref[axis * 162 + k * 9 + f]
                for n in range(len(group)):
                    term = weight * inputs[n][k]
                    sums[n] = term if sums[n] is None else sums[n] + term
            for n, t in enumerate(group):
                store(81 * f + 8 * t, min(8, 81 - 8 * t), sums[n])


def transform(x_ref, a_ref, b_ref, coef_ref, finish):
    def first(index, carry):
        def store(row, count, value):
            a_ref[index, row : row + count, :] = value[:count]

        contract(x_ref, 2 * index, 2 * index + 1, coef_ref, 0, store)
        return carry

    lax.fori_loop(0, 4, first, 0)

    def second(index, carry):
        def store(row, count, value):
            b_ref[index, row : row + count, :] = value[:count]

        contract(a_ref, 2 * index, 2 * index + 1, coef_ref, 1, store)
        return carry

    lax.fori_loop(0, 2, second, 0)
    contract(b_ref, 0, 1, coef_ref, 2, finish)


def dot(left, right):
    return jnp.dot(left, right, preferred_element_type=jnp.float32)


def pack_coarse_kernel(coarse_ref, out_ref):
    boxes = coarse_ref.shape[-1]
    spread = [spread_matrix(boxes, g) for g in range(4)]
    for h in range(2):
        total = dot(coarse_ref[h], spread[0])
        for g in range(1, 4):
            total = total + dot(coarse_ref[2 * g + h], spread[g])
        out_ref[h] = total.astype(jnp.bfloat16)


def pack_waves_kernel(waves_ref, flags_ref, out_ref):
    boxes = waves_ref.shape[-1]
    keep = (1 - flags_ref[...]).astype(jnp.float32)
    source = lax.broadcasted_iota(jnp.int32, (128, SPILL), 0)
    spread = [spread_matrix(boxes, g) for g in range(4)]
    packed_keep = sum(dot(jnp.broadcast_to(keep, (16, boxes)).astype(jnp.bfloat16), s) for s in spread)
    packed_keep = packed_keep[:1]
    for h in range(2):
        total = jnp.zeros((ROWS, 128), jnp.float32)
        for g in range(4):
            if 2 * g + h > 0:
                total = total + dot(waves_ref[2 * g + h - 1], spread[g])
        out_ref[h] = (total * packed_keep).astype(jnp.bfloat16)


def first_kernel(coarse_ref, halo_ref, key_ref, s_ref, spill_ref, x_ref, a_ref, b_ref, coef_ref, fine_ref, *, table):
    boxes = coarse_ref.shape[-1]
    column, octant = local_keys(key_ref, boxes)
    fill_coefficients(coef_ref, octant, table)
    own = pick_own(column, boxes)
    for g in range(4):
        pick = jnp.concatenate([own, pick_spilled(column, g)], 0).astype(jnp.bfloat16)
        for h in range(2):
            both = jnp.concatenate([coarse_ref[2 * g + h], halo_ref[h]], 1)
            x_ref[2 * g + h, 0:ROWS, :] = dot(both, pick)
    fine_ref[ROWS - 1 : 4 * QUARTER, :] = jnp.zeros((4 * QUARTER - ROWS + 1, 128), jnp.float32)

    def store(row, count, value):
        fine_ref[row : row + count, :] = value[:count]

    transform(x_ref, a_ref, b_ref, coef_ref, store)
    fine = fine_ref[...]
    high = fine.astype(jnp.bfloat16)
    low = (fine - high.astype(jnp.float32)).astype(jnp.bfloat16)
    s_ref[0] = high
    s_ref[1] = low
    for part, whole in enumerate((high, low)):
        total = None
        for g in range(4):
            term = dot(whole[QUARTER * g : QUARTER * (g + 1)], spread_matrix(boxes, g))
            total = term if total is None else total + term
        spill_ref[part] = total.astype(jnp.bfloat16)


def second_kernel(
    counts_ref, waves_ref, halo_ref, flags_ref, s_ref, spill_ref, key_ref, code_ref, top_ref,
    x_ref, a_ref, b_ref, coef_ref, value_ref, *, table
):
    boxes = waves_ref.shape[-1]
    column, octant = local_keys(key_ref, boxes)
    fill_coefficients(coef_ref, octant, table)
    own = pick_own(column, boxes)
    keep = (1 - flags_ref[...]).astype(jnp.float32)
    kept = dot(jnp.broadcast_to(keep, (16, boxes)).astype(jnp.bfloat16), own.astype(jnp.bfloat16))
    own_kept = own * kept[:1]
    for g in range(4):
        spilled = pick_spilled(column, g)
        pick = jnp.concatenate([own, spilled], 0).astype(jnp.bfloat16)
        total = None
        for part in range(2):
            both = jnp.concatenate([s_ref[part, QUARTER * g : QUARTER * (g + 1), :], spill_ref[part]], 1)
            term = dot(both, pick)
            total = term if total is None else total + term
        x_ref[0, QUARTER * g : QUARTER * (g + 1), :] = total
        pick = jnp.concatenate([own_kept, spilled], 0).astype(jnp.bfloat16)
        for h in range(2):
            if 2 * g + h > 0:
                both = jnp.concatenate([waves_ref[2 * g + h - 1], halo_ref[h]], 1)
                x_ref[2 * g + h, 0:ROWS, :] = dot(both, pick)
    slot = pl.program_id(0) * 128 + lax.broadcasted_iota(jnp.int32, (8, 128), 1)
    live = jnp.where(slot < counts_ref[0], 1.0, 0.0).astype(jnp.float32)
    padded = value_ref.shape[0]
    value_ref[ROWS - 1 : padded, :] = jnp.zeros((padded - ROWS + 1, 128), jnp.float32)

    def store(row, count, value):
        value_ref[row : row + count, :] = (value * live)[:count]

    transform(x_ref, a_ref, b_ref, coef_ref, store)
    code, top = encode(value_ref[...])
    code_ref[0] = code
    top_ref[0] = jnp.broadcast_to(top, (8, 128))


def encode(value):
    top = jnp.max(jnp.abs(value), axis=0, keepdims=True)
    scaled = value * (32767.0 / jnp.maximum(top, 1e-30))
    return (jnp.round(scaled).astype(jnp.int32).astype(jnp.int16), top)


def decode_square(code, top):
    value = code.astype(jnp.int32).astype(jnp.float32) * (top * np.float32(1.0 / 32767.0))
    return value * value


def reduce_kernel(
    code_ref, top_ref, out_ref, got_code, got_top, mine_code, mine_top, sum_code, sum_top,
    code_send, code_recv, top_send, top_recv, sum_send, sum_recv, peak_send, peak_recv, *, count
):
    tiles, padded = code_ref.shape[:2]
    chunk = padded // count
    me = lax.axis_index("orb")
    barrier = pltpu.get_barrier_semaphore()
    for d in range(1, count):
        pl.semaphore_signal(
            barrier, inc=1, device_id={"orb": lax.rem(me + d, count)}, device_id_type=pl.DeviceIdType.MESH
        )
    pl.semaphore_wait(barrier, count - 1)

    def send(source, target, sends, recvs, d, t):
        copy = pltpu.make_async_remote_copy(
            src_ref=source,
            dst_ref=target.at[d - 1, t],
            send_sem=sends.at[d - 1, t],
            recv_sem=recvs.at[d - 1, t],
            device_id={"orb": lax.rem(me + d, count)},
            device_id_type=pl.DeviceIdType.MESH,
        )
        copy.start()
        return copy

    def rows(owner):
        return pl.ds(pl.multiple_of(owner * chunk, chunk), chunk)

    first, second = ({}, {})
    for t in range(tiles):
        for d in range(1, count):
            peer = lax.rem(me + d, count)
            first[d, t] = (
                send(top_ref.at[t], got_top, top_send, top_recv, d, t),
                send(code_ref.at[t, rows(peer)], got_code, code_send, code_recv, d, t),
            )
    for t in range(tiles):
        total = decode_square(code_ref[t, rows(me), :], top_ref[t, 0:1, :])
        for d in range(1, count):
            for copy in first[d, t]:
                copy.wait_recv()
            total = total + decode_square(got_code[d - 1, t], got_top[d - 1, t, 0:1, :])
        code, top = encode(jnp.sqrt(2.0 * total))
        mine_code[t] = code
        mine_top[t] = jnp.broadcast_to(top, (8, 128))
        out_ref[rows(me), 128 * t : 128 * (t + 1)] = decode_square(code, top)
        for d in range(1, count):
            second[d, t] = (
                send(mine_top.at[t], sum_top, peak_send, peak_recv, d, t),
                send(mine_code.at[t], sum_code, sum_send, sum_recv, d, t),
            )
    for t in range(tiles):
        for d in range(1, count):
            for copy in second[d, t]:
                copy.wait_recv()
            owner = lax.rem(me + count - d, count)
            out_ref[rows(owner), 128 * t : 128 * (t + 1)] = decode_square(
                sum_code[d - 1, t], sum_top[d - 1, t, 0:1, :]
            )
    for pair in list(first.values()) + list(second.values()):
        for copy in pair:
            copy.wait_send()


def transform_scratch():
    return [
        pltpu.VMEM((8, PADDED, 128), jnp.float32),
        pltpu.VMEM((4, PADDED, 128), jnp.float32),
        pltpu.VMEM((2, PADDED, 128), jnp.float32),
        pltpu.VMEM((3 * 162, 8, 128), jnp.float32),
    ]


def shards(coarse, wavelets, leaf_flags, child_key1, child_key2, counts):
    matrix, quad = wavelet_tables()
    valued = np.einsum("kop,gp->kog", matrix, quad)
    boxes = coarse.shape[-1]
    slots = child_key2.shape[0]
    vmem = pl.BlockSpec(memory_space=pltpu.VMEM)
    packed = jax.ShapeDtypeStruct((2, ROWS, 128), jnp.bfloat16)
    coarse, wavelets = coarse[0], wavelets[0]
    params = pltpu.CompilerParams(vmem_limit_bytes=48 * 1024 * 1024)
    coarse_halo = pl.pallas_call(
        pack_coarse_kernel, out_shape=packed, in_specs=[vmem], out_specs=vmem, compiler_params=params
    )(coarse)
    coarse_halo = shifted_2(coarse_halo, "box", 1)
    waves_halo = pl.pallas_call(
        pack_waves_kernel, out_shape=packed, in_specs=[vmem] * 2, out_specs=vmem, compiler_params=params
    )(wavelets, leaf_flags)
    waves_halo = shifted_2(waves_halo, "box", 1)
    scaling, spill = pl.pallas_call(
        lambda *refs: first_kernel(*refs, table=matrix),
        out_shape=(
            jax.ShapeDtypeStruct((2, 4 * QUARTER, 128), jnp.bfloat16),
            jax.ShapeDtypeStruct((2, QUARTER, 128), jnp.bfloat16),
        ),
        in_specs=[vmem] * 3,
        out_specs=(vmem, vmem),
        scratch_shapes=transform_scratch() + [pltpu.VMEM((4 * QUARTER, 128), jnp.float32)],
        compiler_params=params,
    )(coarse, coarse_halo, child_key1.reshape(1, boxes))
    spill = shifted_2(spill, "box", 1)

    def whole(shape):
        return pl.BlockSpec(shape, lambda step: (0,) * len(shape))

    count = lax.axis_size("orb")
    padded = -(-ROWS // (16 * count)) * 16 * count
    chunk = padded // count
    tiles = slots // 128
    codes, tops = pl.pallas_call(
        lambda *refs: second_kernel(*refs, table=valued),
        grid=(tiles,),
        out_shape=(
            jax.ShapeDtypeStruct((tiles, padded, 128), jnp.int16),
            jax.ShapeDtypeStruct((tiles, 8, 128), jnp.float32),
        ),
        in_specs=[
            pl.BlockSpec(memory_space=pltpu.SMEM),
            whole(wavelets.shape),
            whole(packed.shape),
            whole(leaf_flags.shape),
            whole(scaling.shape),
            whole(spill.shape),
            pl.BlockSpec((1, 128), lambda step: (0, step)),
        ],
        out_specs=(
            pl.BlockSpec((1, padded, 128), lambda step: (step, 0, 0)),
            pl.BlockSpec((1, 8, 128), lambda step: (step, 0, 0)),
        ),
        scratch_shapes=transform_scratch() + [pltpu.VMEM((padded, 128), jnp.float32)],
        compiler_params=params,
    )(counts, wavelets, waves_halo, leaf_flags, scaling, spill, child_key2.reshape(1, slots))
    peers = (count - 1, tiles)
    density = pl.pallas_call(
        lambda *refs: reduce_kernel(*refs, count=count),
        out_shape=jax.ShapeDtypeStruct((padded, slots), jnp.float32),
        in_specs=[vmem] * 2,
        out_specs=vmem,
        scratch_shapes=[
            pltpu.VMEM(peers + (chunk, 128), jnp.int16),
            pltpu.VMEM(peers + (8, 128), jnp.float32),
            pltpu.VMEM((tiles, chunk, 128), jnp.int16),
            pltpu.VMEM((tiles, 8, 128), jnp.float32),
            pltpu.VMEM(peers + (chunk, 128), jnp.int16),
            pltpu.VMEM(peers + (8, 128), jnp.float32),
        ]
        + [pltpu.SemaphoreType.DMA(peers)] * 8,
        compiler_params=pltpu.CompilerParams(collective_id=0, has_side_effects=True),
    )(codes, tops)
    return density[:ROWS]


def solution(mesh):
    in_specs = (
        P("orb", None, None, "box"),
        P("orb", None, None, "box"),
        P("orb", "box"),
        P("box"),
        P("box"),
        P("box"),
    )
    out_specs = P(None, "box")
    return jax.shard_map(shards, mesh=mesh, in_specs=in_specs, out_specs=out_specs, check_vma=False)
```

```python
import math

import jax
import jax.numpy as jnp
import numpy as np
from jax import lax
from jax.experimental import pallas as pl
from jax.experimental.pallas import tpu as pltpu
from jax.sharding import PartitionSpec as P

SPILL = 32


def legendre_pair(order, where):
    before = where * 0.0 + 1.0
    value = where
    for degree in range(1, order):
        before, value = (value, ((2 * degree + 1) * where * value - degree * before) / (degree + 1))
    return (value, before)


def gauss_rule(order):
    nodes = np.cos(np.pi * (np.arange(order) + 0.75) / (order + 0.5))
    for repeat in range(40):
        value, before = legendre_pair(order, nodes)
        slope = order * (nodes * value - before) / (nodes * nodes - 1.0)
        nodes = nodes - value / slope
    value, before = legendre_pair(order, nodes)
    slope = order * (nodes * value - before) / (nodes * nodes - 1.0)
    weights = 2.0 / ((1.0 - nodes * nodes) * slope * slope)
    return (nodes[::-1], weights[::-1])


def legendre_basis(where):
    shifted = 2.0 * where - 1.0
    rows = [shifted * 0.0 + 1.0, shifted]
    for degree in range(1, 8):
        rows.append(
            ((2 * degree + 1) * shifted * rows[degree] - degree * rows[degree - 1]) / (degree + 1)
        )
    scale = np.sqrt(2.0 * np.arange(9) + 1.0)[:, None]
    return np.stack(rows, 0) * scale


def complement_rows(scaling_rows):
    members = [scaling_rows[index] for index in range(9)]
    kept = []
    identity = np.eye(18)
    for column in range(18):
        vector = identity[column]
        for passes in range(2):
            for member in members + kept:
                vector = vector - np.dot(member, vector) * member
        length = np.sqrt(np.dot(vector, vector))
        if length > 0.1 and len(kept) < 9:
            kept.append(vector / length)
    return np.stack(kept, 0)


def wavelet_tables():
    nodes, weights = gauss_rule(24)
    points = 0.5 * (nodes + 1.0)
    halves = 0.5 * weights
    lower = legendre_basis(0.5 * points) * halves @ legendre_basis(points).T / math.sqrt(2.0)
    upper = legendre_basis(0.5 * points + 0.5) * halves @ legendre_basis(points).T / math.sqrt(2.0)
    scaling_rows = np.concatenate([lower, upper], 1)
    wavelet_rows = complement_rows(scaling_rows)
    matrix = np.concatenate([scaling_rows, wavelet_rows], 0).reshape(2, 9, 2, 9)
    gauss, gauss_weights = gauss_rule(9)
    quad = legendre_basis(0.5 * (gauss + 1.0)).T * np.sqrt(0.5 * gauss_weights)[:, None]
    return (matrix.reshape(18, 2, 9), quad)


ROWS = 729
PADDED = 800
GROUPS = ((0, 1), (2, 3), (4, 5), (6, 7), (8, 9, 10))
QUARTER = 192


def local_keys(keys, boxes):
    key = keys - lax.axis_index("box") * (8 * boxes)
    return (lax.shift_right_arithmetic(key, 3), key & 7)


def spread_matrix(boxes, group):
    source = lax.broadcasted_iota(jnp.int32, (boxes, 128), 0)
    target = lax.broadcasted_iota(jnp.int32, (boxes, 128), 1)
    hit = (source - (boxes - SPILL) == target - SPILL * group) & (source >= boxes - SPILL)
    return hit.astype(jnp.float32).astype(jnp.bfloat16)


def pick_own(column, boxes):
    row = lax.broadcasted_iota(jnp.int32, (boxes, column.shape[1]), 0)
    return (row == column).astype(jnp.float32)


def pick_spilled(column, group):
    row = lax.broadcasted_iota(jnp.int32, (128, column.shape[1]), 0)
    hit = (row == column + SPILL * (group + 1)) & (column < 0)
    return hit.astype(jnp.float32)


def fill_coefficients(coef_ref, octant, table):
    for axis in range(3):
        bit = jnp.broadcast_to((octant >> axis) & 1, (8, 128)) == 1
        for k in range(18):
            for f in range(9):
                coef_ref[axis * 162 + k * 9 + f] = jnp.where(
                    bit, np.float32(table[k, 1, f]), np.float32(table[k, 0, f])
                )


def contract(source_ref, low, high, coef_ref, axis, store):
    for group in GROUPS:
        inputs = [
            [
                source_ref[block, pl.ds(l + 72 * t, 8, stride=9), :]
                for block in (low, high)
                for l in range(9)
            ]
            for t in group
        ]
        for f in range(9):
            sums = [None] * len(group)
            for k in range(18):
                weight = coef_ref[axis * 162 + k * 9 + f]
                for n in range(len(group)):
                    term = weight * inputs[n][k]
                    sums[n] = term if sums[n] is None else sums[n] + term
            for n, t in enumerate(group):
                store(81 * f + 8 * t, min(8, 81 - 8 * t), sums[n])


def lower_axis(source_ref, target_ref, coef_ref, axis, start, stop):
    def step(index, carry):
        def store(row, count, value):
            target_ref[index, row : row + count, :] = value[:count]

        contract(source_ref, 2 * index, 2 * index + 1, coef_ref, axis, store)
        return carry

    lax.fori_loop(start, stop, step, 0)


def dot(left, right):
    return jnp.dot(left, right, preferred_element_type=jnp.float32)


def encode(value):
    top = jnp.max(jnp.abs(value), axis=0, keepdims=True)
    scaled = value * (32767.0 / jnp.maximum(top, 1e-30))
    return (jnp.round(scaled).astype(jnp.int32).astype(jnp.int16), top)


def decode_square(code, top):
    value = code.astype(jnp.int32).astype(jnp.float32) * (top * np.float32(1.0 / 32767.0))
    return value * value


def density_kernel(
    counts_ref, coarse_hbm, waves_hbm, flags_ref, key1_ref, key2_ref, out_ref,
    coarse_ref, waves_ref, pack_ref, halo_ref, fine_ref, spill_ref, spilled_ref,
    x_ref, a_ref, b_ref, coef_ref, value_ref, code_ref, top_ref,
    got_code, got_top, mine_code, mine_top, sum_code, sum_top,
    load_sem, halo_send, halo_recv, code_send, code_recv, top_send, top_recv,
    sum_send, sum_recv, peak_send, peak_recv, *, count, ranges, table, valued
):
    boxes = coarse_ref.shape[-1]
    tiles, padded = code_ref.shape[:2]
    chunk = padded // count
    me, position = lax.axis_index("orb"), lax.axis_index("box")
    after, before = lax.rem(position + 1, ranges), lax.rem(position + ranges - 1, ranges)
    mesh_id = pl.DeviceIdType.MESH
    load_coarse = pltpu.make_async_copy(coarse_hbm, coarse_ref, load_sem.at[0])
    load_waves = pltpu.make_async_copy(waves_hbm, waves_ref, load_sem.at[1])
    load_coarse.start()
    load_waves.start()
    barrier = pltpu.get_barrier_semaphore()
    for d in range(1, count):
        pl.semaphore_signal(barrier, inc=1, device_id={"orb": lax.rem(me + d, count)}, device_id_type=mesh_id)
    for other in (after, before):
        pl.semaphore_signal(barrier, inc=1, device_id={"box": other}, device_id_type=mesh_id)

    def halo(source, target, index):
        return pltpu.make_async_remote_copy(
            src_ref=source,
            dst_ref=target,
            send_sem=halo_send.at[index],
            recv_sem=halo_recv.at[index],
            device_id={"box": after},
            device_id_type=mesh_id,
        )

    def direct(source, target, sends, recvs, d, t):
        return pltpu.make_async_remote_copy(
            src_ref=source,
            dst_ref=target.at[d - 1, t],
            send_sem=sends.at[d - 1, t],
            recv_sem=recvs.at[d - 1, t],
            device_id={"orb": lax.rem(me + d, count)},
            device_id_type=mesh_id,
        )

    def rows(owner):
        return pl.ds(pl.multiple_of(owner * chunk, chunk), chunk)

    def partials(d, t):
        peer = lax.rem(me + d, count)
        return (
            direct(top_ref.at[t], got_top, top_send, top_recv, d, t),
            direct(code_ref.at[t, rows(peer)], got_code, code_send, code_recv, d, t),
        )

    def totals(d, t):
        return (
            direct(mine_top.at[t], sum_top, peak_send, peak_recv, d, t),
            direct(mine_code.at[t], sum_code, sum_send, sum_recv, d, t),
        )

    coarse_halo = halo(pack_ref.at[0], halo_ref.at[0], 0)
    waves_halo = halo(pack_ref.at[1], halo_ref.at[1], 1)
    fine_halo = halo(spill_ref, spilled_ref, 2)
    keep = jnp.broadcast_to((1 - flags_ref[...]).astype(jnp.float32), (16, boxes)).astype(jnp.bfloat16)
    spread = [spread_matrix(boxes, g) for g in range(4)]
    load_coarse.wait()
    for h in range(2):
        total = dot(coarse_ref[0, h], spread[0])
        for g in range(1, 4):
            total = total + dot(coarse_ref[0, 2 * g + h], spread[g])
        pack_ref[0, h] = total.astype(jnp.bfloat16)
    pl.semaphore_wait(barrier, count + 1)
    coarse_halo.start()
    load_waves.wait()
    packed_keep = sum(dot(keep, s) for s in spread)[:1]
    for h in range(2):
        total = None
        for g in range(4):
            if 2 * g + h > 0:
                term = dot(waves_ref[0, 2 * g + h - 1], spread[g])
                total = term if total is None else total + term
        pack_ref[1, h] = (total * packed_keep).astype(jnp.bfloat16)
    column, octant = local_keys(key1_ref[...], boxes)
    fill_coefficients(coef_ref, octant, table)
    own = pick_own(column, boxes)
    waves_halo.start()
    fine_ref[ROWS - 1 : 4 * QUARTER, :] = jnp.zeros((4 * QUARTER - ROWS + 1, 128), jnp.float32)
    value_ref[ROWS - 1 : padded, :] = jnp.zeros((padded - ROWS + 1, 128), jnp.float32)
    coarse_halo.wait_recv()
    for g in range(4):
        pick = jnp.concatenate([own, pick_spilled(column, g)], 0).astype(jnp.bfloat16)
        for h in range(2):
            both = jnp.concatenate([coarse_ref[0, 2 * g + h], halo_ref[0, h]], 1)
            x_ref[2 * g + h, 0:ROWS, :] = dot(both, pick)
    lower_axis(x_ref, a_ref, coef_ref, 0, 0, 4)
    lower_axis(a_ref, b_ref, coef_ref, 1, 0, 2)

    def store_fine(row, rows_in, value):
        fine_ref[row : row + rows_in, :] = value[:rows_in]

    contract(b_ref, 0, 1, coef_ref, 2, store_fine)
    for part in range(2):
        total = None
        for g in range(4):
            quarter = fine_ref[QUARTER * g : QUARTER * (g + 1), :]
            half = quarter.astype(jnp.bfloat16)
            if part == 1:
                half = (quarter - half.astype(jnp.float32)).astype(jnp.bfloat16)
            term = dot(half, spread[g])
            total = term if total is None else total + term
        spill_ref[part] = total.astype(jnp.bfloat16)
    fine_halo.start()

    def leaf_tile(t, carry):
        column, octant = local_keys(key2_ref[t], boxes)
        fill_coefficients(coef_ref, octant, valued)
        own = pick_own(column, boxes)
        own_kept = own * dot(keep, own.astype(jnp.bfloat16))[:1]

        @pl.when(t == 0)
        def arrived_waves():
            waves_halo.wait_recv()

        for g in range(4):
            pick = jnp.concatenate([own_kept, pick_spilled(column, g)], 0).astype(jnp.bfloat16)
            for h in range(2):
                if 2 * g + h > 0:
                    both = jnp.concatenate([waves_ref[0, 2 * g + h - 1], halo_ref[1, h]], 1)
                    x_ref[2 * g + h, 0:ROWS, :] = dot(both, pick)
        lower_axis(x_ref, a_ref, coef_ref, 0, 1, 4)

        @pl.when(t == 0)
        def arrived_fine():
            fine_halo.wait_recv()

        for g in range(4):
            pick = jnp.concatenate([own, pick_spilled(column, g)], 0).astype(jnp.bfloat16)
            quarter = fine_ref[QUARTER * g : QUARTER * (g + 1), :]
            high = quarter.astype(jnp.bfloat16)
            low = (quarter - high.astype(jnp.float32)).astype(jnp.bfloat16)
            total = dot(jnp.concatenate([high, spilled_ref[0]], 1), pick)
            total = total + dot(jnp.concatenate([low, spilled_ref[1]], 1), pick)
            x_ref[0, QUARTER * g : QUARTER * (g + 1), :] = total
        lower_axis(x_ref, a_ref, coef_ref, 0, 0, 1)
        lower_axis(a_ref, b_ref, coef_ref, 1, 0, 2)
        slot = t * 128 + lax.broadcasted_iota(jnp.int32, (8, 128), 1)
        live = jnp.where(slot < counts_ref[0], 1.0, 0.0).astype(jnp.float32)

        def store_value(row, rows_in, value):
            value_ref[row : row + rows_in, :] = (value * live)[:rows_in]

        contract(b_ref, 0, 1, coef_ref, 2, store_value)
        code, top = encode(value_ref[...])
        code_ref[t] = code
        top_ref[t] = jnp.broadcast_to(top, (8, 128))
        for d in range(1, count):
            for copy in partials(d, t):
                copy.start()
        return carry

    lax.fori_loop(0, tiles, leaf_tile, 0)
    for t in range(tiles):
        total = decode_square(code_ref[t, rows(me), :], top_ref[t, 0:1, :])
        for d in range(1, count):
            for copy in partials(d, t):
                copy.wait_recv()
            total = total + decode_square(got_code[d - 1, t], got_top[d - 1, t, 0:1, :])
        code, top = encode(jnp.sqrt(2.0 * total))
        mine_code[t] = code
        mine_top[t] = jnp.broadcast_to(top, (8, 128))
        out_ref[rows(me), 128 * t : 128 * (t + 1)] = decode_square(code, top)
        for d in range(1, count):
            for copy in totals(d, t):
                copy.start()
    for t in range(tiles):
        for d in range(1, count):
            for copy in totals(d, t):
                copy.wait_recv()
            owner = lax.rem(me + count - d, count)
            out_ref[rows(owner), 128 * t : 128 * (t + 1)] = decode_square(
                sum_code[d - 1, t], sum_top[d - 1, t, 0:1, :]
            )
    for copy in (coarse_halo, waves_halo, fine_halo):
        copy.wait_send()
    for t in range(tiles):
        for d in range(1, count):
            for copy in partials(d, t) + totals(d, t):
                copy.wait_send()


def shards(coarse, wavelets, leaf_flags, child_key1, child_key2, counts):
    matrix, quad = wavelet_tables()
    valued = np.einsum("kop,gp->kog", matrix, quad)
    boxes = coarse.shape[-1]
    slots = child_key2.shape[0]
    count, ranges = lax.axis_size("orb"), lax.axis_size("box")
    padded = -(-ROWS // (16 * count)) * 16 * count
    chunk = padded // count
    tiles = slots // 128
    peers = (count - 1, tiles)
    vmem = pl.BlockSpec(memory_space=pltpu.VMEM)
    anywhere = pl.BlockSpec(memory_space=pl.ANY)
    density = pl.pallas_call(
        lambda *refs: density_kernel(*refs, count=count, ranges=ranges, table=matrix, valued=valued),
        out_shape=jax.ShapeDtypeStruct((padded, slots), jnp.float32),
        in_specs=[pl.BlockSpec(memory_space=pltpu.SMEM), anywhere, anywhere, vmem, vmem, vmem],
        out_specs=vmem,
        scratch_shapes=[
            pltpu.VMEM(coarse.shape, jnp.bfloat16),
            pltpu.VMEM(wavelets.shape, jnp.bfloat16),
            pltpu.VMEM((2, 2, ROWS, 128), jnp.bfloat16),
            pltpu.VMEM((2, 2, ROWS, 128), jnp.bfloat16),
            pltpu.VMEM((4 * QUARTER, 128), jnp.float32),
            pltpu.VMEM((2, QUARTER, 128), jnp.bfloat16),
            pltpu.VMEM((2, QUARTER, 128), jnp.bfloat16),
            pltpu.VMEM((8, PADDED, 128), jnp.float32),
            pltpu.VMEM((4, PADDED, 128), jnp.float32),
            pltpu.VMEM((2, PADDED, 128), jnp.float32),
            pltpu.VMEM((3 * 162, 8, 128), jnp.float32),
            pltpu.VMEM((padded, 128), jnp.float32),
            pltpu.VMEM((tiles, padded, 128), jnp.int16),
            pltpu.VMEM((tiles, 8, 128), jnp.float32),
            pltpu.VMEM(peers + (chunk, 128), jnp.int16),
            pltpu.VMEM(peers + (8, 128), jnp.float32),
            pltpu.VMEM((tiles, chunk, 128), jnp.int16),
            pltpu.VMEM((tiles, 8, 128), jnp.float32),
            pltpu.VMEM(peers + (chunk, 128), jnp.int16),
            pltpu.VMEM(peers + (8, 128), jnp.float32),
            pltpu.SemaphoreType.DMA((2,)),
            pltpu.SemaphoreType.DMA((3,)),
            pltpu.SemaphoreType.DMA((3,)),
        ]
        + [pltpu.SemaphoreType.DMA(peers)] * 8,
        compiler_params=pltpu.CompilerParams(
            collective_id=0, has_side_effects=True, vmem_limit_bytes=60 * 1024 * 1024
        ),
    )(
        counts,
        coarse,
        wavelets,
        leaf_flags,
        child_key1.reshape(1, boxes),
        child_key2.reshape(tiles, 1, 128),
    )
    return density[:ROWS]


def solution(mesh):
    in_specs = (
        P("orb", None, None, "box"),
        P("orb", None, None, "box"),
        P("orb", "box"),
        P("box"),
        P("box"),
        P("box"),
    )
    out_specs = P(None, "box")
    return jax.shard_map(shards, mesh=mesh, in_specs=in_specs, out_specs=out_specs, check_vma=False)
```

```python
import math

import jax
import jax.numpy as jnp
import numpy as np
from jax import lax
from jax.experimental import pallas as pl
from jax.experimental.pallas import tpu as pltpu
from jax.sharding import PartitionSpec as P

SPILL = 32


def legendre_pair(order, where):
    before = where * 0.0 + 1.0
    value = where
    for degree in range(1, order):
        before, value = (value, ((2 * degree + 1) * where * value - degree * before) / (degree + 1))
    return (value, before)


def gauss_rule(order):
    nodes = np.cos(np.pi * (np.arange(order) + 0.75) / (order + 0.5))
    for repeat in range(40):
        value, before = legendre_pair(order, nodes)
        slope = order * (nodes * value - before) / (nodes * nodes - 1.0)
        nodes = nodes - value / slope
    value, before = legendre_pair(order, nodes)
    slope = order * (nodes * value - before) / (nodes * nodes - 1.0)
    weights = 2.0 / ((1.0 - nodes * nodes) * slope * slope)
    return (nodes[::-1], weights[::-1])


def legendre_basis(where):
    shifted = 2.0 * where - 1.0
    rows = [shifted * 0.0 + 1.0, shifted]
    for degree in range(1, 8):
        rows.append(
            ((2 * degree + 1) * shifted * rows[degree] - degree * rows[degree - 1]) / (degree + 1)
        )
    scale = np.sqrt(2.0 * np.arange(9) + 1.0)[:, None]
    return np.stack(rows, 0) * scale


def complement_rows(scaling_rows):
    members = [scaling_rows[index] for index in range(9)]
    kept = []
    identity = np.eye(18)
    for column in range(18):
        vector = identity[column]
        for passes in range(2):
            for member in members + kept:
                vector = vector - np.dot(member, vector) * member
        length = np.sqrt(np.dot(vector, vector))
        if length > 0.1 and len(kept) < 9:
            kept.append(vector / length)
    return np.stack(kept, 0)


def wavelet_tables():
    nodes, weights = gauss_rule(24)
    points = 0.5 * (nodes + 1.0)
    halves = 0.5 * weights
    lower = legendre_basis(0.5 * points) * halves @ legendre_basis(points).T / math.sqrt(2.0)
    upper = legendre_basis(0.5 * points + 0.5) * halves @ legendre_basis(points).T / math.sqrt(2.0)
    scaling_rows = np.concatenate([lower, upper], 1)
    wavelet_rows = complement_rows(scaling_rows)
    matrix = np.concatenate([scaling_rows, wavelet_rows], 0).reshape(2, 9, 2, 9)
    gauss, gauss_weights = gauss_rule(9)
    quad = legendre_basis(0.5 * (gauss + 1.0)).T * np.sqrt(0.5 * gauss_weights)[:, None]
    return (matrix.reshape(18, 2, 9), quad)


ROWS = 729
PADDED = 800
SEGMENT = 92
HALVES = (((0, 1), (2, 3, 4)), ((5, 6), (7, 8), (9, 10)))
GROUPS = ((0, 1), (2, 3), (4, 5), (6, 7), (8, 9, 10))
QUARTER = 192


def local_keys(keys, boxes):
    key = keys - lax.axis_index("box") * (8 * boxes)
    return (lax.shift_right_arithmetic(key, 3), key & 7)


def spread_matrix(boxes, group):
    source = lax.broadcasted_iota(jnp.int32, (boxes, 128), 0)
    target = lax.broadcasted_iota(jnp.int32, (boxes, 128), 1)
    hit = (source - (boxes - SPILL) == target - SPILL * group) & (source >= boxes - SPILL)
    return hit.astype(jnp.float32).astype(jnp.bfloat16)


def pick_own(column, boxes):
    row = lax.broadcasted_iota(jnp.int32, (boxes, column.shape[1]), 0)
    return (row == column).astype(jnp.float32)


def pick_spilled(column, group):
    row = lax.broadcasted_iota(jnp.int32, (128, column.shape[1]), 0)
    hit = (row == column + SPILL * (group + 1)) & (column < 0)
    return hit.astype(jnp.float32)


def fill_coefficients(coef_ref, octant, table):
    for axis in range(3):
        bit = jnp.broadcast_to((octant >> axis) & 1, (8, 128)) == 1
        for k in range(18):
            for f in range(9):
                coef_ref[axis * 162 + k * 9 + f] = jnp.where(
                    bit, np.float32(table[k, 1, f]), np.float32(table[k, 0, f])
                )


def contract(source_ref, low, high, coef_ref, axis, store, groups=GROUPS):
    def load(block, row):
        if len(source_ref.shape) == 2:
            return source_ref[pl.ds(8 * row + block, 8, stride=72), :]
        return source_ref[block, pl.ds(row, 8, stride=9), :]

    for group in groups:
        inputs = [[load(block, l + 72 * t) for block in (low, high) for l in range(9)] for t in group]
        for f in range(9):
            sums = [None] * len(group)
            for k in range(18):
                weight = coef_ref[axis * 162 + k * 9 + f]
                for n in range(len(group)):
                    term = weight * inputs[n][k]
                    sums[n] = term if sums[n] is None else sums[n] + term
            for n, t in enumerate(group):
                store(81 * f + 8 * t, min(8, 81 - 8 * t), sums[n])


def lower_axis(source_ref, target_ref, coef_ref, axis, start, stop, groups=GROUPS):
    def step(index, carry):
        def store(row, count, value):
            target_ref[index, row : row + count, :] = value[:count]

        contract(source_ref, 2 * index, 2 * index + 1, coef_ref, axis, store, groups)
        return carry

    lax.fori_loop(start, stop, step, 0)


def dot(left, right):
    return jnp.dot(left, right, preferred_element_type=jnp.float32)


def encode(value):
    top = jnp.max(jnp.abs(value), axis=0, keepdims=True)
    scaled = value * (32767.0 / jnp.maximum(top, 1e-30))
    return (jnp.round(scaled).astype(jnp.int32).astype(jnp.int16), top)


def decode_square(code, top):
    value = code.astype(jnp.int32).astype(jnp.float32) * (top * np.float32(1.0 / 32767.0))
    return value * value


def density_kernel(
    counts_ref, coarse_hbm, waves_hbm, flags_ref, key1_ref, key2_ref, sum_code, sum_top,
    coarse_ref, waves_ref, coarse_pack_ref, coarse_halo_ref, pack_ref, halo_ref, level_ref, fine_ref, spill_ref, spilled_ref,
    x_ref, a_ref, b_ref, coef_ref, value_ref, code_ref, top_ref,
    got_code, got_top, load_sem, halo_send, halo_recv, code_send, code_recv, top_send, top_recv,
    sum_send, sum_recv, peak_send, peak_recv, *, count, ranges, table, valued
):
    boxes = coarse_hbm.shape[-1]
    tiles, padded = code_ref.shape[:2]
    chunk = padded // count
    me, position = lax.axis_index("orb"), lax.axis_index("box")
    after, before = lax.rem(position + 1, ranges), lax.rem(position + ranges - 1, ranges)
    mesh_id = pl.DeviceIdType.MESH
    load_coarse = pltpu.make_async_copy(coarse_hbm, coarse_ref.at[pl.ds(0, ROWS)], load_sem.at[0])
    load_waves = pltpu.make_async_copy(waves_hbm, waves_ref, load_sem.at[1])
    load_coarse.start()
    load_waves.start()
    barrier = pltpu.get_barrier_semaphore()
    for d in range(1, count):
        pl.semaphore_signal(barrier, inc=1, device_id={"orb": lax.rem(me + d, count)}, device_id_type=mesh_id)
    for other in (after, before):
        pl.semaphore_signal(barrier, inc=1, device_id={"box": other}, device_id_type=mesh_id)

    def halo(source, target, index):
        return pltpu.make_async_remote_copy(
            src_ref=source,
            dst_ref=target,
            send_sem=halo_send.at[index],
            recv_sem=halo_recv.at[index],
            device_id={"box": after},
            device_id_type=mesh_id,
        )

    def direct(source, target, sends, recvs, d, t):
        return pltpu.make_async_remote_copy(
            src_ref=source,
            dst_ref=target,
            send_sem=sends.at[d - 1, t],
            recv_sem=recvs.at[d - 1, t],
            device_id={"orb": lax.rem(me + d, count)},
            device_id_type=mesh_id,
        )

    def rows(owner):
        return pl.ds(pl.multiple_of(owner * chunk, chunk), chunk)

    def partials(d, t):
        peer = lax.rem(me + d, count)
        return (
            direct(top_ref.at[t], got_top.at[d - 1, t], top_send, top_recv, d, t),
            direct(code_ref.at[t, rows(peer)], got_code.at[d - 1, t], code_send, code_recv, d, t),
        )

    def totals(d, t):
        return (
            direct(sum_top.at[me, t], sum_top.at[me, t], peak_send, peak_recv, d, t),
            direct(sum_code.at[me, t], sum_code.at[me, t], sum_send, sum_recv, d, t),
        )

    coarse_halo = [halo(coarse_pack_ref.at[h], coarse_halo_ref.at[h], h) for h in range(2)]
    waves_halo = halo(pack_ref, halo_ref, 2)
    fine_halo = halo(spill_ref, spilled_ref, 3)
    keep = jnp.broadcast_to((1 - flags_ref[...]).astype(jnp.float32), (16, boxes)).astype(jnp.bfloat16)
    spread = [spread_matrix(boxes, g) for g in range(4)]
    tail = 8 * SEGMENT - ROWS
    coarse_ref[ROWS : ROWS + tail] = jnp.zeros((tail, 8, boxes), jnp.bfloat16)

    def segment(index):
        return coarse_ref[SEGMENT * index : SEGMENT * (index + 1)].reshape(8 * SEGMENT, boxes)

    load_coarse.wait()
    for h in range(2):
        total = dot(segment(4 * h), spread[0])
        for g in range(1, 4):
            total = total + dot(segment(4 * h + g), spread[g])
        coarse_pack_ref[h] = total.astype(jnp.bfloat16)
        if h == 0:
            pl.semaphore_wait(barrier, count + 1)
        coarse_halo[h].start()
    load_waves.wait()
    packed_keep = sum(dot(keep, s) for s in spread)[:1]
    for h in range(2):
        total = None
        for g in range(4):
            if 4 * h + g > 0:
                term = dot(waves_ref[0, 4 * h + g - 1], spread[g])
                total = term if total is None else total + term
        pack_ref[h] = (total * packed_keep).astype(jnp.bfloat16)
    waves_halo.start()
    column, octant = local_keys(key1_ref[...], boxes)
    fill_coefficients(coef_ref.at[tiles], octant, table)
    own = pick_own(column, boxes)
    fine_ref[ROWS - 1 : 4 * QUARTER, :] = jnp.zeros((4 * QUARTER - ROWS + 1, 128), jnp.float32)
    value_ref[ROWS - 1 : padded, :] = jnp.zeros((padded - ROWS + 1, 128), jnp.float32)

    def leaf_coefficients(t, carry):
        fill_coefficients(coef_ref.at[t], local_keys(key2_ref[t], boxes)[1], valued)
        return carry

    lax.fori_loop(0, tiles, leaf_coefficients, 0)
    coef = coef_ref.at[tiles]
    for h in range(2):
        coarse_halo[h].wait_recv()
        for g in range(4):
            pick = jnp.concatenate([own, pick_spilled(column, g)], 0).astype(jnp.bfloat16)
            both = jnp.concatenate([segment(4 * h + g), coarse_halo_ref[h]], 1)
            start = 8 * SEGMENT * (4 * h + g)
            level_ref[start : start + 8 * SEGMENT, :] = dot(both, pick)
        lower_axis(level_ref, a_ref, coef, 0, 0, 4, HALVES[h])
    lower_axis(a_ref, b_ref, coef, 1, 0, 2)

    def store_fine(row, rows_in, value):
        fine_ref[row : row + rows_in, :] = value[:rows_in]

    contract(b_ref, 0, 1, coef, 2, store_fine)
    for part in range(2):
        total = None
        for g in range(4):
            quarter = fine_ref[QUARTER * g : QUARTER * (g + 1), :]
            half = quarter.astype(jnp.bfloat16)
            if part == 1:
                half = (quarter - half.astype(jnp.float32)).astype(jnp.bfloat16)
            term = dot(half, spread[g])
            total = term if total is None else total + term
        spill_ref[part] = total.astype(jnp.bfloat16)
    fine_halo.start()

    def leaf_tile(t, carry):
        column = local_keys(key2_ref[t], boxes)[0]
        coef = coef_ref.at[t]
        own = pick_own(column, boxes)
        own_kept = own * dot(keep, own.astype(jnp.bfloat16))[:1]

        @pl.when(t == 0)
        def arrived_waves():
            waves_halo.wait_recv()

        for g in range(4):
            pick = jnp.concatenate([own_kept, pick_spilled(column, g)], 0).astype(jnp.bfloat16)
            for h in range(2):
                if 4 * h + g > 0:
                    both = jnp.concatenate([waves_ref[0, 4 * h + g - 1], halo_ref[h]], 1)
                    x_ref[4 * h + g, 0:ROWS, :] = dot(both, pick)
        lower_axis(x_ref, a_ref, coef, 0, 1, 4)

        @pl.when(t == 0)
        def arrived_fine():
            fine_halo.wait_recv()

        for g in range(4):
            pick = jnp.concatenate([own, pick_spilled(column, g)], 0).astype(jnp.bfloat16)
            quarter = fine_ref[QUARTER * g : QUARTER * (g + 1), :]
            high = quarter.astype(jnp.bfloat16)
            low = (quarter - high.astype(jnp.float32)).astype(jnp.bfloat16)
            total = dot(jnp.concatenate([high, spilled_ref[0]], 1), pick)
            total = total + dot(jnp.concatenate([low, spilled_ref[1]], 1), pick)
            x_ref[0, QUARTER * g : QUARTER * (g + 1), :] = total
        lower_axis(x_ref, a_ref, coef, 0, 0, 1)
        lower_axis(a_ref, b_ref, coef, 1, 0, 2)
        slot = t * 128 + lax.broadcasted_iota(jnp.int32, (8, 128), 1)
        live = jnp.where(slot < counts_ref[0], 1.0, 0.0).astype(jnp.float32)

        def store_value(row, rows_in, value):
            value_ref[row : row + rows_in, :] = (value * live)[:rows_in]

        contract(b_ref, 0, 1, coef, 2, store_value)
        code, top = encode(value_ref[...])
        code_ref[t] = code
        top_ref[t] = jnp.broadcast_to(top, (8, 128))
        for d in range(1, count):
            for copy in partials(d, t):
                copy.start()
        return carry

    lax.fori_loop(0, tiles, leaf_tile, 0)
    for t in range(tiles):
        total = decode_square(code_ref[t, rows(me), :], top_ref[t, 0:1, :])
        for d in range(1, count):
            for copy in partials(d, t):
                copy.wait_recv()
            total = total + decode_square(got_code[d - 1, t], got_top[d - 1, t, 0:1, :])
        code, top = encode(jnp.sqrt(2.0 * total))
        sum_code[me, t] = code
        sum_top[me, t] = jnp.broadcast_to(top, (8, 128))
        for d in range(1, count):
            for copy in totals(d, t):
                copy.start()
    for t in range(tiles):
        for d in range(1, count):
            for copy in totals(d, t):
                copy.wait_recv()
    for copy in (*coarse_halo, waves_halo, fine_halo):
        copy.wait_send()
    for t in range(tiles):
        for d in range(1, count):
            for copy in partials(d, t) + totals(d, t):
                copy.wait_send()


def decode_kernel(code_ref, top_ref, out_ref):
    count, tiles, chunk = code_ref.shape[:3]
    for owner in range(count):
        rows = min(chunk, ROWS - owner * chunk)
        if rows > 0:
            for t in range(tiles):
                value = decode_square(code_ref[owner, t], top_ref[owner, t, 0:1, :])
                out_ref[owner * chunk : owner * chunk + rows, 128 * t : 128 * (t + 1)] = value[:rows]


def shards(coarse, wavelets, leaf_flags, child_key1, child_key2, counts):
    matrix, quad = wavelet_tables()
    valued = np.einsum("kop,gp->kog", matrix, quad)
    boxes = coarse.shape[-1]
    slots = child_key2.shape[0]
    count, ranges = lax.axis_size("orb"), lax.axis_size("box")
    padded = -(-ROWS // (16 * count)) * 16 * count
    chunk = padded // count
    tiles = slots // 128
    peers = (count - 1, tiles)
    vmem = pl.BlockSpec(memory_space=pltpu.VMEM)
    anywhere = pl.BlockSpec(memory_space=pltpu.HBM)
    codes, tops = pl.pallas_call(
        lambda *refs: density_kernel(*refs, count=count, ranges=ranges, table=matrix, valued=valued),
        out_shape=(
            jax.ShapeDtypeStruct((count, tiles, chunk, 128), jnp.int16),
            jax.ShapeDtypeStruct((count, tiles, 8, 128), jnp.float32),
        ),
        in_specs=[pl.BlockSpec(memory_space=pltpu.SMEM), anywhere, anywhere, vmem, vmem, vmem],
        out_specs=(vmem, vmem),
        scratch_shapes=[
            pltpu.VMEM((8 * SEGMENT, 8, boxes), jnp.bfloat16),
            pltpu.VMEM(wavelets.shape, jnp.bfloat16),
            pltpu.VMEM((2, 8 * SEGMENT, 128), jnp.bfloat16),
            pltpu.VMEM((2, 8 * SEGMENT, 128), jnp.bfloat16),
            pltpu.VMEM((2, ROWS, 128), jnp.bfloat16),
            pltpu.VMEM((2, ROWS, 128), jnp.bfloat16),
            pltpu.VMEM((8 * PADDED, 128), jnp.float32),
            pltpu.VMEM((4 * QUARTER, 128), jnp.float32),
            pltpu.VMEM((2, QUARTER, 128), jnp.bfloat16),
            pltpu.VMEM((2, QUARTER, 128), jnp.bfloat16),
            pltpu.VMEM((8, PADDED, 128), jnp.float32),
            pltpu.VMEM((4, PADDED, 128), jnp.float32),
            pltpu.VMEM((2, PADDED, 128), jnp.float32),
            pltpu.VMEM((tiles + 1, 3 * 162, 8, 128), jnp.float32),
            pltpu.VMEM((padded, 128), jnp.float32),
            pltpu.VMEM((tiles, padded, 128), jnp.int16),
            pltpu.VMEM((tiles, 8, 128), jnp.float32),
            pltpu.VMEM(peers + (chunk, 128), jnp.int16),
            pltpu.VMEM(peers + (8, 128), jnp.float32),
            pltpu.SemaphoreType.DMA((2,)),
            pltpu.SemaphoreType.DMA((4,)),
            pltpu.SemaphoreType.DMA((4,)),
        ]
        + [pltpu.SemaphoreType.DMA(peers)] * 8,
        compiler_params=pltpu.CompilerParams(
            collective_id=0, has_side_effects=True, vmem_limit_bytes=60 * 1024 * 1024
        ),
    )(
        counts,
        jnp.transpose(coarse[0], (1, 0, 2)),
        wavelets,
        leaf_flags,
        child_key1.reshape(1, boxes),
        child_key2.reshape(tiles, 1, 128),
    )
    return pl.pallas_call(
        decode_kernel,
        out_shape=jax.ShapeDtypeStruct((ROWS, slots), jnp.float32),
        in_specs=[vmem] * 2,
        out_specs=vmem,
    )(codes, tops)


def solution(mesh):
    in_specs = (
        P("orb", None, None, "box"),
        P("orb", None, None, "box"),
        P("orb", "box"),
        P("box"),
        P("box"),
        P("box"),
    )
    out_specs = P(None, "box")
    return jax.shard_map(shards, mesh=mesh, in_specs=in_specs, out_specs=out_specs, check_vma=False)
```
